32 devices in a mesh: gx: 4 (over x, core), gy: 8 (over z, y).
Axes of the slice: x: 2, y: 2, z: 4, core: 2. Of those that a mesh axis runs over, the one named last changes fastest.
Arguments:
- tracers: float32 [4, 2, 64, 384], P(None, None, 'gx', 'gy'), may hold values from 0.05 to 2
- velocity: float32 [2, 64, 384], P(None, 'gx', 'gy'), may hold values from -1.75 to 1.75
- land_mask: int32 [64, 384], P('gx', 'gy'), may hold values 0 or 1
- diffusivity: float32 [2], replicated, may hold values from 0.02 to 0.15
- bio_rates: float32 [7, 2], replicated, may hold values from 0.2 to 1
Outputs:
- updated: float32 [4, 2, 64, 384], P(None, None, 'gx', 'gy')
The draws below stay inside these ranges and needn't reach their ends.
All inputs are finite; a program needn't handle non-finite values. No bound on the sum of `land_mask` on one device may be relied on, other than what follows from the above.
Results may differ from the reference program's by a relative error of at most 0.00002.
Values sent between devices are 32-bit elements; how exact they have to be, the bound alone decides.
A program may use at most 64 MiB of HBM per device.

```python
import math
import jax
import jax.numpy as jnp
import numpy as np

TILE = 16
LEV = 2
TRACERS = 4
SLOTS = 3
ROWS = 64
SCOLS = 384
N_GX = 4
N_GY = 8


def touch_ends(values, own_key, smallest, top_value):
    place = [jax.random.randint(jax.random.fold_in(own_key, axis), (), 0, length) for axis, length in enumerate(values.shape)]
    longest = values.shape.index(max(values.shape))
    beside = place[:longest] + [(place[longest] + 1) % values.shape[longest]] + place[longest + 1:]
    return values.at[tuple(place)].set(smallest).at[tuple(beside)].set(top_value)


def block_levels(own_key, dims, cuts, least, top_value):
    loudness = 1.0
    for dim, blocks in cuts:
        draws = jax.random.uniform(jax.random.fold_in(jax.random.fold_in(own_key, 6), dim), (blocks,), jnp.float32, least / len(cuts), top_value / len(cuts))
        loudness = loudness * jnp.repeat(jnp.exp(draws), dims[dim] // blocks).reshape((-1,) + (1,) * (len(dims) - 1 - dim))
    return loudness


def normal_values(stream_key, shape, width, reach, shards=(), kind=jnp.bfloat16):
    entries = width * jax.random.normal(stream_key, shape, jnp.float32)
    if shards:
        entries = entries * block_levels(stream_key, shape, shards, -0.22, 0.18)
    return jnp.clip(entries, -reach, reach).astype(kind)


def setup_inputs(seed: int = 0) -> dict:
    key_of = jax.random.split(jax.random.key(seed), 6)
    tracers = jnp.clip(jnp.exp(math.log(2.0) - 3.6888794 * jax.random.uniform(key_of[0], (TRACERS, LEV, ROWS, SCOLS), jnp.float32) ** block_levels(key_of[0], (TRACERS, LEV, ROWS, SCOLS), ((2, 4), (3, 8)), -0.2, 0.2)), 0.05, 2.0)
    velocity = normal_values(key_of[1], (2, ROWS, SCOLS), 0.12, 1.75, ((1, 4), (2, 8)), jnp.float32)
    land_mask = touch_ends((jax.random.randint(key_of[2], (ROWS, SCOLS), 0, 5) < 4).astype(jnp.int32), jax.random.fold_in(key_of[2], 1), 0, 1)
    diffusivity = jnp.clip(jnp.exp(jax.random.uniform(key_of[3], (LEV,), jnp.float32, math.log(0.02), math.log(0.15))), 0.02, 0.15)
    bio_rates = jnp.clip(jnp.exp(jax.random.uniform(key_of[4], (7, LEV), jnp.float32, math.log(0.2), math.log(1.0))), 0.2, 1.0)
    return dict(tracers=tracers, velocity=velocity, land_mask=land_mask, diffusivity=diffusivity, bio_rates=bio_rates)


step_size = 0.5
assimilated = 0.3
SEAM_TABLE = (((4, 1, 0), (5, 0, 0), (3, 3, 0), (1, 2, 0)),
              ((4, 3, 1), (5, 3, 0), (0, 3, 0), (2, 2, 0)),
              ((4, 0, 1), (5, 1, 1), (1, 3, 0), (3, 2, 0)),
              ((4, 2, 0), (5, 2, 1), (2, 3, 0), (0, 2, 0)),
              ((2, 0, 1), (0, 0, 0), (3, 0, 0), (1, 0, 1)),
              ((0, 1, 0), (2, 1, 1), (3, 1, 1), (1, 1, 0)))


def inner_strip(square, border):
    if border == 0:
        return square[..., :2, :]
    if border == 1:
        return jnp.flip(square[..., -2:, :], -2)
    if border == 2:
        return jnp.swapaxes(square[..., :, :2], -1, -2)
    return jnp.swapaxes(jnp.flip(square[..., :, -2:], -1), -1, -2)


def turn_velocity(ribbon, own_side, their_side, flipped):
    tracer_rows = ribbon.shape[-3] - 3
    col_speed = ribbon[..., tracer_rows, :, :]
    row_speed = ribbon[..., tracer_rows + 1, :, :]
    normal = -jnp.where(their_side == 0, -row_speed, jnp.where(their_side == 1, row_speed, jnp.where(their_side == 2, -col_speed, col_speed)))
    tangent = jnp.where(their_side < 2, col_speed, row_speed)
    tangent = jnp.where(flipped, -tangent, tangent)
    fresh_col = jnp.where(own_side < 2, tangent, jnp.where(own_side == 2, -normal, normal))
    fresh_row = jnp.where(own_side == 0, -normal, jnp.where(own_side == 1, normal, tangent))
    ribbon = ribbon.at[..., tracer_rows, :, :].set(fresh_col)
    return ribbon.at[..., tracer_rows + 1, :, :].set(fresh_row)


def frame(center, northern, southern, western, eastern):
    field_count, extent = center.shape[0], center.shape[-1]
    padded = jnp.zeros((field_count, extent + 4, extent + 4), center.dtype)
    padded = padded.at[:, 2:-2, 2:-2].set(center)
    padded = padded.at[:, :2, 2:-2].set(jnp.flip(northern, 1))
    padded = padded.at[:, -2:, 2:-2].set(southern)
    padded = padded.at[:, 2:-2, :2].set(jnp.swapaxes(jnp.flip(western, 1), 1, 2))
    padded = padded.at[:, 2:-2, -2:].set(jnp.swapaxes(eastern, 1, 2))
    return padded


def face_flux(behind, current, beyond, further, face_speed):
    lowest = jnp.minimum(current, beyond)
    highest = jnp.maximum(current, beyond)
    rising = jnp.clip((5.0 * current + 2.0 * beyond - behind) / 6.0, lowest, highest)
    falling = jnp.clip((5.0 * beyond + 2.0 * current - further) / 6.0, lowest, highest)
    return jnp.maximum(face_speed, 0.0) * rising + jnp.minimum(face_speed, 0.0) * falling


def tendency(padded, diffusivity, bio_rates):
    tracer_rows = padded.shape[0] - 3
    levels = diffusivity.shape[0]
    extent = padded.shape[-1] - 4
    amounts = padded[:tracer_rows]
    along_col = padded[tracer_rows]
    along_row = padded[tracer_rows + 1]
    wet_mask = padded[tracer_rows + 2]
    mixing = jnp.tile(diffusivity, tracer_rows // levels)[:, None, None]
    middle = slice(2, 2 + extent)
    wall_x = wet_mask[middle, 1:extent + 2] * wet_mask[middle, 2:extent + 3]
    speed_x = 0.5 * (along_col[middle, 1:extent + 2] + along_col[middle, 2:extent + 3]) * wall_x
    flux_x = face_flux(amounts[:, middle, 0:extent + 1], amounts[:, middle, 1:extent + 2], amounts[:, middle, 2:extent + 3], amounts[:, middle, 3:extent + 4], speed_x)
    spread_x = mixing * wall_x * (amounts[:, middle, 2:extent + 3] - amounts[:, middle, 1:extent + 2])
    wall_y = wet_mask[1:extent + 2, middle] * wet_mask[2:extent + 3, middle]
    speed_y = 0.5 * (along_row[1:extent + 2, middle] + along_row[2:extent + 3, middle]) * wall_y
    flux_y = face_flux(amounts[:, 0:extent + 1, middle], amounts[:, 1:extent + 2, middle], amounts[:, 2:extent + 3, middle], amounts[:, 3:extent + 4, middle], speed_y)
    spread_y = mixing * wall_y * (amounts[:, 2:extent + 3, middle] - amounts[:, 1:extent + 2, middle])
    transport = flux_x[:, :, :-1] - flux_x[:, :, 1:] + spread_x[:, :, 1:] - spread_x[:, :, :-1]
    transport = transport + flux_y[:, :-1, :] - flux_y[:, 1:, :] + spread_y[:, 1:, :] - spread_y[:, :-1, :]
    center = amounts[:, middle, middle].reshape(tracer_rows // levels, levels, extent, extent)
    growth, half_nutrient, grazing_rate, half_phyto, phyto_loss, grazer_loss, recycling = [bio_rates[number][:, None, None] for number in range(7)]
    nutrient, phytoplankton, grazer, detritus = center[0], center[1], center[2], center[3]
    uptake = growth * phytoplankton * nutrient * nutrient / (half_nutrient * half_nutrient + nutrient * nutrient)
    grazing = grazing_rate * grazer * phytoplankton * phytoplankton / (half_phyto * half_phyto + phytoplankton * phytoplankton)
    phyto_death = phyto_loss * phytoplankton
    crowding = grazer_loss * grazer * grazer
    returned = recycling * detritus
    biology = jnp.stack([returned - uptake, uptake - grazing - phyto_death, assimilated * grazing - crowding, (1.0 - assimilated) * grazing + phyto_death + crowding - returned]).reshape(tracer_rows, extent, extent)
    return (transport + biology) * wet_mask[middle, middle]


def column_places():
    all_columns = 6 * N_GX
    places = []
    for column in range(all_columns):
        holder = column * N_GY // all_columns
        places.append(holder * SLOTS + column - (holder * all_columns + N_GY - 1) // N_GY)
    return places


def reference(tracers, velocity, land_mask, diffusivity, bio_rates):
    extent = TILE * N_GX
    places = column_places()
    column_index = np.array([[places[face * N_GX + cell // TILE] * TILE + cell % TILE for cell in range(extent)] for face in range(6)], np.int32)
    statics = jnp.concatenate([velocity, land_mask.astype(jnp.float32)[None]], 0)
    amounts = tracers.reshape(TRACERS * LEV, extent, tracers.shape[-1])

    def to_faces(layout):
        return jnp.stack([layout[:, :, column_index[face]] for face in range(6)])

    initial = to_faces(amounts)
    fixed_faces = to_faces(statics)

    def rate(current_faces):
        stacked_fields = jnp.concatenate([current_faces, fixed_faces], 1)
        pieces = []
        for face in range(6):
            ghosts = []
            for border in range(4):
                their_face, their_side, flipped = SEAM_TABLE[face][border]
                ribbon = inner_strip(stacked_fields[their_face], their_side)
                if flipped:
                    ribbon = jnp.flip(ribbon, -1)
                ghosts.append(turn_velocity(ribbon, border, their_side, flipped == 1))
            pieces.append(tendency(frame(stacked_fields[face], ghosts[0], ghosts[1], ghosts[2], ghosts[3]), diffusivity, bio_rates))
        return jnp.stack(pieces)

    sectioned = initial + step_size * rate(initial)
    second_section = sectioned + step_size * rate(sectioned)
    averaged = 0.5 * (initial + second_section)
    result = jnp.zeros(amounts.shape, jnp.float32)
    for face in range(6):
        result = result.at[:, :, column_index[face]].set(averaged[face])
    return result.reshape(tracers.shape)
```

```python
import functools

import jax
import jax.numpy as jnp
from jax import lax
from jax.experimental import pallas as pl
from jax.experimental.pallas import tpu as pltpu
from jax.sharding import PartitionSpec as P

step_size = 0.5
assimilated = 0.3
SEAM_TABLE = (
    ((4, 1, 0), (5, 0, 0), (3, 3, 0), (1, 2, 0)),
    ((4, 3, 1), (5, 3, 0), (0, 3, 0), (2, 2, 0)),
    ((4, 0, 1), (5, 1, 1), (1, 3, 0), (3, 2, 0)),
    ((4, 2, 0), (5, 2, 1), (2, 3, 0), (0, 2, 0)),
    ((2, 0, 1), (0, 0, 0), (3, 0, 0), (1, 0, 1)),
    ((0, 1, 0), (2, 1, 1), (3, 1, 1), (1, 1, 0)),
)
DEPTH = 2


def neighbours(gx, gy, gx_count, gy_count, slot_count):
    side_tiles = gx_count
    all_columns = 6 * side_tiles
    first = lax.div(gy * all_columns + gy_count - 1, gy_count)
    used = lax.div((gy + 1) * all_columns + gy_count - 1, gy_count) - first
    table = []
    for slot in range(slot_count):
        column = jnp.minimum(first + slot, all_columns - 1)
        face = lax.div(column, side_tiles)
        b = column - face * side_tiles
        row = []
        for edge in range(4):
            codes = [t[edge][0] * 8 + t[edge][1] * 2 + t[edge][2] for t in SEAM_TABLE]
            code = jnp.int32(codes[5])
            for f in range(5):
                code = jnp.where(face == f, jnp.int32(codes[f]), code)
            t_face = lax.shift_right_logical(code, jnp.int32(3))
            t_side = lax.shift_right_logical(code, jnp.int32(1)) & 3
            t_flip = code & 1
            along = b if edge < 2 else gx
            t_along = jnp.where(t_flip == 1, side_tiles - 1 - along, along)
            t_far = jnp.where((t_side & 1) == 1, side_tiles - 1, 0)
            t_row = jnp.where(t_side < 2, t_far, t_along)
            t_col = jnp.where(t_side < 2, t_along, t_far)
            if edge == 0:
                inside, i_row, i_col = gx > 0, gx - 1, b
            elif edge == 1:
                inside, i_row, i_col = gx < side_tiles - 1, gx + 1, b
            elif edge == 2:
                inside, i_row, i_col = b > 0, gx, b - 1
            else:
                inside, i_row, i_col = b < side_tiles - 1, gx, b + 1
            t_row = jnp.where(inside, i_row, t_row)
            t_column = jnp.where(inside, face * side_tiles + i_col, t_face * side_tiles + t_col)
            t_edge = jnp.where(inside, edge ^ 1, t_side)
            flip = jnp.where(inside, 0, t_flip)
            t_gy = lax.div(t_column * gy_count, all_columns)
            t_slot = t_column - lax.div(t_gy * all_columns + gy_count - 1, gy_count)
            valid = slot < used
            local = (t_row == gx) & (t_gy == gy)
            row.append((t_row, t_gy, t_slot, t_edge, flip, valid, local))
        table.append(row)
    return used, table


def kernel(
    gx_count, gy_count, slots, species, levels, tile,
    tr_hbm, vel_hbm, land_hbm, dif_hbm, bio_hbm, out,
    tr, vel, land, dif, bio,
    wide, rows, vrows, pad, vpad, opad, ups, downs, mixes, faces,
    send1, recv1, send2, recv2,
    in_sem, send_sem, recv_sem,
):
    gx, gy = lax.axis_index("gx"), lax.axis_index("gy")
    nf = species * levels
    lanes = nf * tile
    breadth = slots * tile
    loads = [
        pltpu.make_async_copy(src, dst, in_sem.at[i])
        for i, (src, dst) in enumerate(
            ((tr_hbm, tr), (vel_hbm, vel), (land_hbm, land), (dif_hbm, dif), (bio_hbm, bio))
        )
    ]
    for load in loads:
        load.start()
    used, table = neighbours(gx, gy, gx_count, gy_count, slots)
    barrier = pltpu.get_barrier_semaphore()
    count = jnp.int32(0)
    for slot in range(slots):
        for edge in range(4):
            t_row, t_gy, _, _, _, valid, local = table[slot][edge]
            remote = valid & ~local
            count = count + jnp.where(remote, 1, 0)

            @pl.when(remote)
            def _():
                pl.semaphore_signal(
                    barrier, inc=1, device_id=(t_row, t_gy),
                    device_id_type=pl.DeviceIdType.MESH,
                )
    for load in loads:
        load.wait()

    lane = lax.broadcasted_iota(jnp.int32, (tile, lanes), 1)
    block = lane // tile
    backward = block * tile + (tile - 1) - lane % tile

    def roll(x, shift):
        return x if shift % lanes == 0 else pltpu.roll(x, shift % lanes, 1)

    def reverse(x):
        return jnp.take_along_axis(x, backward, axis=1)

    def to_rows(fields):
        result = []
        for slot in range(slots):
            acc = roll(fields[0], -slot * tile)
            for f in range(1, len(fields)):
                acc = jnp.where(block == f, roll(fields[f], f * tile - slot * tile), acc)
            result.append(acc)
        return result

    def from_rows(per_slot, f):
        acc = roll(per_slot[0], -f * tile)
        for slot in range(1, slots):
            acc = jnp.where(block == slot, roll(per_slot[slot], slot * tile - f * tile), acc)
        return acc

    def to_cols(stacked):
        turned = stacked.T
        return [turned[s * tile:(s + 1) * tile] for s in range(slots)]

    def split(stacked):
        return [stacked[f * tile:(f + 1) * tile] for f in range(nf)]

    def exchange(stage, send, recv, fill):
        for slot in range(slots):
            for edge in range(4):
                t_row, t_gy, t_slot, t_edge, flip, valid, local = table[slot][edge]
                fill(send, slot, edge, flip)

                @pl.when(valid & ~local)
                def _():
                    pltpu.make_async_remote_copy(
                        src_ref=send.at[slot, edge], dst_ref=recv.at[t_slot, t_edge],
                        send_sem=send_sem.at[stage, slot, edge],
                        recv_sem=recv_sem.at[stage, t_slot, t_edge],
                        device_id=(t_row, t_gy), device_id_type=pl.DeviceIdType.MESH,
                    ).start()

                @pl.when(valid & local)
                def _():
                    recv[t_slot, t_edge] = send[slot, edge]

                @pl.when(~valid)
                def _():
                    recv[slot, edge] = jnp.zeros(recv.shape[2:], jnp.float32)

    def arrive(stage, send, recv):
        for slot in range(slots):
            for edge in range(4):
                t_row, t_gy, _, _, _, valid, local = table[slot][edge]

                @pl.when(valid & ~local)
                def _():
                    copy = pltpu.make_async_remote_copy(
                        src_ref=send.at[slot, edge], dst_ref=recv.at[slot, edge],
                        send_sem=send_sem.at[stage, slot, edge],
                        recv_sem=recv_sem.at[stage, slot, edge],
                        device_id=(t_row, t_gy), device_id_type=pl.DeviceIdType.MESH,
                    )
                    copy.wait_send()
                    copy.wait_recv()

    def lay(stacked):
        both = (to_rows(split(stacked)), to_cols(stacked))
        for way in range(2):
            for slot in range(slots):
                x = both[way][slot]
                rows[0, way, slot] = x
                rows[1, way, slot] = reverse(x)
                pad[way, slot, DEPTH:DEPTH + tile] = x

    def fill_tracers(send, slot, edge, flip):
        way, far = edge // 2, edge % 2
        for depth in range(DEPTH):
            at = tile - 1 - depth if far else depth
            send[slot, edge, depth:depth + 1] = rows[flip, way, slot, at:at + 1]

    def fill_all(send, slot, edge, flip):
        fill_tracers(send, slot, edge, flip)
        way, far = edge // 2, edge % 2
        at = tile - 1 if far else 0
        speed = vrows[0, flip, way, slot, at:at + 1]
        send[slot, edge, DEPTH:DEPTH + 1] = speed if far else -speed
        send[slot, edge, DEPTH + 1:DEPTH + 2] = vrows[1, flip, way, slot, at:at + 1]

    def ghosts(recv):
        for way in range(2):
            for slot in range(slots):
                for far in range(2):
                    for depth in range(DEPTH):
                        at = DEPTH + tile + depth if far else DEPTH - 1 - depth
                        pad[way, slot, at:at + 1] = recv[slot, 2 * way + far, depth:depth + 1]

    wide[...] = jnp.zeros(wide.shape, jnp.float32)
    wide[0:nf * tile, 0:breadth] = tr[...]
    first = wide[0:nf * tile]
    lay(first)
    for i in range(2):
        wide[(nf + i) * tile:(nf + i + 1) * tile, 0:breadth] = vel[i]
    wide[(nf + 2) * tile:(nf + 3) * tile, 0:breadth] = land[...].astype(jnp.float32)
    along_col = wide[nf * tile:(nf + 1) * tile]
    along_row = wide[(nf + 1) * tile:(nf + 2) * tile]
    ocean = wide[(nf + 2) * tile:(nf + 3) * tile]
    for kind, (by_row, by_col) in enumerate(((along_row, along_col), (ocean, ocean))):
        both = (to_rows([by_row] * nf), to_cols(jnp.concatenate([by_col] * nf, 0)))
        for way in range(2):
            for slot in range(slots):
                x = both[way][slot]
                vrows[kind, 0, way, slot] = x
                vrows[kind, 1, way, slot] = reverse(x)
                (vpad, opad)[kind][way, slot, DEPTH:DEPTH + tile] = x

    pl.semaphore_wait(barrier, count)
    exchange(0, send1, recv1, fill_all)

    def biology(fields):
        result = [None] * nf
        for level in range(levels):
            n, p, z, d = (fields[t * levels + level] for t in range(4))
            g, kn, r, kp, lp, lz, m = (bio[k, level] for k in range(7))
            uptake = g * p * n * n / (kn * kn + n * n)
            grazing = r * z * p * p / (kp * kp + p * p)
            death = lp * p
            crowding = lz * z * z
            returned = m * d
            result[level] = returned - uptake
            result[levels + level] = uptake - grazing - death
            result[2 * levels + level] = assimilated * grazing - crowding
            result[3 * levels + level] = (1.0 - assimilated) * grazing + death + crowding - returned
        return result

    def rate(stacked, sources):
        by_way = []
        for way in range(2):
            per_slot = []
            for slot in range(slots):
                behind = pad[way, slot, 0:tile + 1]
                current = pad[way, slot, 1:tile + 2]
                beyond = pad[way, slot, 2:tile + 3]
                further = pad[way, slot, 3:tile + 4]
                low, high = jnp.minimum(current, beyond), jnp.maximum(current, beyond)
                rising = (5.0 * current + 2.0 * beyond - behind) * (1.0 / 6.0)
                falling = (5.0 * beyond + 2.0 * current - further) * (1.0 / 6.0)
                rising = jnp.minimum(jnp.maximum(rising, low), high)
                falling = jnp.minimum(jnp.maximum(falling, low), high)
                flux = ups[way, slot, 0:tile + 1] * rising + downs[way, slot, 0:tile + 1] * falling
                faces[way, slot, 0:tile + 1] = flux - mixes[way, slot, 0:tile + 1] * (beyond - current)
                per_slot.append(faces[way, slot, 0:tile] - faces[way, slot, 1:tile + 1])
            by_way.append(per_slot)
        cols = by_way[1] + [jnp.zeros((lanes - breadth, lanes), jnp.float32)]
        turned = split(jnp.concatenate(cols, 0).T)
        return [
            (turned[f] + from_rows(by_way[0], f) + sources[f]) * ocean for f in range(nf)
        ]

    sources = biology(split(first))
    arrive(0, send1, recv1)
    ghosts(recv1)
    level_of = lax.broadcasted_iota(jnp.int32, (tile + 1, lanes), 1) // tile % levels
    mixing = jnp.full((tile + 1, lanes), dif[0], jnp.float32)
    for level in range(1, levels):
        mixing = jnp.where(level_of == level, dif[level], mixing)
    for way in range(2):
        for slot in range(slots):
            for far in range(2):
                at = DEPTH + tile if far else DEPTH - 1
                sent = recv1[slot, 2 * way + far, DEPTH:DEPTH + 1]
                vpad[way, slot, at:at + 1] = -sent if far else sent
                opad[way, slot, at:at + 1] = recv1[slot, 2 * way + far, DEPTH + 1:DEPTH + 2]
            wall = opad[way, slot, 1:tile + 2] * opad[way, slot, 2:tile + 3]
            speed = 0.5 * (vpad[way, slot, 1:tile + 2] + vpad[way, slot, 2:tile + 3]) * wall
            ups[way, slot, 0:tile + 1] = jnp.maximum(speed, 0.0)
            downs[way, slot, 0:tile + 1] = jnp.minimum(speed, 0.0)
            mixes[way, slot, 0:tile + 1] = mixing * wall
    rates = rate(first, sources)
    sectioned = first + step_size * jnp.concatenate(rates, 0)
    lay(sectioned)
    exchange(1, send2, recv2, fill_tracers)
    sources = biology(split(sectioned))
    arrive(1, send2, recv2)
    ghosts(recv2)
    rates = rate(sectioned, sources)
    second = sectioned + step_size * jnp.concatenate(rates, 0)
    averaged = 0.5 * (first + second)
    held = lax.broadcasted_iota(jnp.int32, averaged.shape, 1) // tile < used
    averaged = jnp.where(held, averaged, 0.0)
    out[...] = averaged[:, 0:breadth]


def shards(gx_count, gy_count, tracers, velocity, land_mask, diffusivity, bio_rates):
    species, levels, tile, breadth = tracers.shape
    slots = breadth // tile
    nf = species * levels
    lanes = nf * tile
    height = tile + 2 * DEPTH + 4
    both = (2, slots, height, lanes)
    f32 = jnp.float32
    out = pl.pallas_call(
        functools.partial(kernel, gx_count, gy_count, slots, species, levels, tile),
        out_shape=jax.ShapeDtypeStruct((nf * tile, breadth), f32),
        in_specs=[pl.BlockSpec(memory_space=pl.ANY)] * 5,
        out_specs=pl.BlockSpec(memory_space=pltpu.VMEM),
        scratch_shapes=[
            pltpu.VMEM((nf * tile, breadth), f32),
            pltpu.VMEM((2, tile, breadth), f32),
            pltpu.VMEM((tile, breadth), jnp.int32),
            pltpu.SMEM((levels,), f32),
            pltpu.SMEM((7, levels), f32),
            pltpu.VMEM(((nf + 3) * tile, lanes), f32),
            pltpu.VMEM((2, 2, slots, tile, lanes), f32),
            pltpu.VMEM((2, 2, 2, slots, tile, lanes), f32),
            pltpu.VMEM(both, f32),
            pltpu.VMEM(both, f32),
            pltpu.VMEM(both, f32),
            pltpu.VMEM(both, f32),
            pltpu.VMEM(both, f32),
            pltpu.VMEM(both, f32),
            pltpu.VMEM(both, f32),
            pltpu.VMEM((slots, 4, DEPTH + 2, lanes), f32),
            pltpu.VMEM((slots, 4, DEPTH + 2, lanes), f32),
            pltpu.VMEM((slots, 4, DEPTH, lanes), f32),
            pltpu.VMEM((slots, 4, DEPTH, lanes), f32),
            pltpu.SemaphoreType.DMA((5,)),
            pltpu.SemaphoreType.DMA((2, slots, 4)),
            pltpu.SemaphoreType.DMA((2, slots, 4)),
        ],
        compiler_params=pltpu.CompilerParams(collective_id=0, has_side_effects=True),
        name="tracer_step",
    )(tracers.reshape(nf * tile, breadth), velocity, land_mask, diffusivity, bio_rates)
    return out.reshape(tracers.shape)


def solution(mesh):
    return jax.shard_map(
        functools.partial(shards, mesh.shape["gx"], mesh.shape["gy"]),
        mesh=mesh,
        in_specs=(P(None, None, "gx", "gy"), P(None, "gx", "gy"), P("gx", "gy"), P(), P()),
        out_specs=P(None, None, "gx", "gy"),
        check_vma=False,
    )
```

```python
import functools

import jax
import jax.numpy as jnp
from jax import lax
from jax.experimental import pallas as pl
from jax.experimental.pallas import tpu as pltpu
from jax.sharding import PartitionSpec as P

step_size = 0.5
assimilated = 0.3
SEAM_TABLE = (
    ((4, 1, 0), (5, 0, 0), (3, 3, 0), (1, 2, 0)),
    ((4, 3, 1), (5, 3, 0), (0, 3, 0), (2, 2, 0)),
    ((4, 0, 1), (5, 1, 1), (1, 3, 0), (3, 2, 0)),
    ((4, 2, 0), (5, 2, 1), (2, 3, 0), (0, 2, 0)),
    ((2, 0, 1), (0, 0, 0), (3, 0, 0), (1, 0, 1)),
    ((0, 1, 0), (2, 1, 1), (3, 1, 1), (1, 1, 0)),
)
DEPTH = 2


def neighbours(gx, gy, gx_count, gy_count, slot_count):
    side_tiles = gx_count
    all_columns = 6 * side_tiles
    first = lax.div(gy * all_columns + gy_count - 1, gy_count)
    used = lax.div((gy + 1) * all_columns + gy_count - 1, gy_count) - first
    table = []
    for slot in range(slot_count):
        column = jnp.minimum(first + slot, all_columns - 1)
        face = lax.div(column, side_tiles)
        b = column - face * side_tiles
        row = []
        for edge in range(4):
            codes = [t[edge][0] * 8 + t[edge][1] * 2 + t[edge][2] for t in SEAM_TABLE]
            code = jnp.int32(codes[5])
            for f in range(5):
                code = jnp.where(face == f, jnp.int32(codes[f]), code)
            t_face = lax.shift_right_logical(code, jnp.int32(3))
            t_side = lax.shift_right_logical(code, jnp.int32(1)) & 3
            t_flip = code & 1
            along = b if edge < 2 else gx
            t_along = jnp.where(t_flip == 1, side_tiles - 1 - along, along)
            t_far = jnp.where((t_side & 1) == 1, side_tiles - 1, 0)
            t_row = jnp.where(t_side < 2, t_far, t_along)
            t_col = jnp.where(t_side < 2, t_along, t_far)
            if edge == 0:
                inside, i_row, i_col = gx > 0, gx - 1, b
            elif edge == 1:
                inside, i_row, i_col = gx < side_tiles - 1, gx + 1, b
            elif edge == 2:
                inside, i_row, i_col = b > 0, gx, b - 1
            else:
                inside, i_row, i_col = b < side_tiles - 1, gx, b + 1
            t_row = jnp.where(inside, i_row, t_row)
            t_column = jnp.where(inside, face * side_tiles + i_col, t_face * side_tiles + t_col)
            t_edge = jnp.where(inside, edge ^ 1, t_side)
            flip = jnp.where(inside, 0, t_flip)
            t_gy = lax.div(t_column * gy_count, all_columns)
            t_slot = t_column - lax.div(t_gy * all_columns + gy_count - 1, gy_count)
            valid = slot < used
            local = (t_row == gx) & (t_gy == gy)
            row.append((t_row, t_gy, t_slot, t_edge, flip, valid, local))
        table.append(row)
    return used, table


def kernel(
    gx_count, gy_count, slots, species, levels, tile,
    tr_hbm, vel_hbm, land_hbm, dif_hbm, bio_hbm, out,
    tr, vel, land, dif, bio,
    wide, rows, vrows, pad, vpad, opad, ups, downs, mixes, faces,
    send1, recv1, send2, recv2,
    in_sem, send_sem, recv_sem,
):
    gx, gy = lax.axis_index("gx"), lax.axis_index("gy")
    nf = species * levels
    lanes = nf * tile
    breadth = slots * tile
    loads = [
        pltpu.make_async_copy(src, dst, in_sem.at[i])
        for i, (src, dst) in enumerate(
            ((tr_hbm, tr), (vel_hbm, vel), (land_hbm, land), (dif_hbm, dif), (bio_hbm, bio))
        )
    ]
    for load in loads:
        load.start()
    used, table = neighbours(gx, gy, gx_count, gy_count, slots)
    barrier = pltpu.get_barrier_semaphore()
    count = jnp.int32(0)
    for slot in range(slots):
        for edge in range(4):
            t_row, t_gy, _, _, _, valid, local = table[slot][edge]
            remote = valid & ~local
            count = count + jnp.where(remote, 1, 0)

            @pl.when(remote)
            def _():
                pl.semaphore_signal(
                    barrier, inc=1, device_id=(t_row, t_gy),
                    device_id_type=pl.DeviceIdType.MESH,
                )
    for load in loads:
        load.wait()

    lane = lax.broadcasted_iota(jnp.int32, (tile, lanes), 1)
    block = lane // tile
    backward = block * tile + (tile - 1) - lane % tile

    def roll(x, shift):
        return x if shift % lanes == 0 else pltpu.roll(x, shift % lanes, 1)

    def reverse(x):
        return jnp.take_along_axis(x, backward, axis=1)

    def to_rows(fields):
        result = []
        for slot in range(slots):
            acc = roll(fields[0], -slot * tile)
            for f in range(1, len(fields)):
                acc = jnp.where(block == f, roll(fields[f], f * tile - slot * tile), acc)
            result.append(acc)
        return result

    def from_rows(per_slot, f):
        acc = roll(per_slot[0], -f * tile)
        for slot in range(1, slots):
            acc = jnp.where(block == slot, roll(per_slot[slot], slot * tile - f * tile), acc)
        return acc

    def to_cols(stacked):
        turned = stacked.T
        return [turned[s * tile:(s + 1) * tile] for s in range(slots)]

    def split(stacked):
        return [stacked[f * tile:(f + 1) * tile] for f in range(nf)]

    def exchange(stage, send, recv, fill):
        for slot in range(slots):
            for edge in range(4):
                t_row, t_gy, t_slot, t_edge, flip, valid, local = table[slot][edge]
                fill(send, slot, edge, flip)

                @pl.when(valid & ~local)
                def _():
                    pltpu.make_async_remote_copy(
                        src_ref=send.at[slot, edge], dst_ref=recv.at[t_slot, t_edge],
                        send_sem=send_sem.at[stage, slot, edge],
                        recv_sem=recv_sem.at[stage, t_slot, t_edge],
                        device_id=(t_row, t_gy), device_id_type=pl.DeviceIdType.MESH,
                    ).start()

                @pl.when(valid & local)
                def _():
                    recv[t_slot, t_edge] = send[slot, edge]

                @pl.when(~valid)
                def _():
                    recv[slot, edge] = jnp.zeros(recv.shape[2:], jnp.float32)

    def arrive(stage, send, recv, sent=False):
        for slot in range(slots):
            for edge in range(4):
                t_row, t_gy, _, _, _, valid, local = table[slot][edge]

                @pl.when(valid & ~local)
                def _():
                    copy = pltpu.make_async_remote_copy(
                        src_ref=send.at[slot, edge], dst_ref=recv.at[slot, edge],
                        send_sem=send_sem.at[stage, slot, edge],
                        recv_sem=recv_sem.at[stage, slot, edge],
                        device_id=(t_row, t_gy), device_id_type=pl.DeviceIdType.MESH,
                    )
                    if sent:
                        copy.wait_send()
                    else:
                        copy.wait_recv()

    def lay(stacked):
        both = (to_rows(split(stacked)), to_cols(stacked))
        for way in range(2):
            for slot in range(slots):
                x = both[way][slot]
                rows[0, way, slot] = x
                rows[1, way, slot] = reverse(x)
                pad[way, slot, DEPTH:DEPTH + tile] = x

    def fill_tracers(send, slot, edge, flip):
        way, far = edge // 2, edge % 2
        for depth in range(DEPTH):
            at = tile - 1 - depth if far else depth
            send[slot, edge, depth:depth + 1] = rows[flip, way, slot, at:at + 1]

    def fill_all(send, slot, edge, flip):
        fill_tracers(send, slot, edge, flip)
        way, far = edge // 2, edge % 2
        at = tile - 1 if far else 0
        speed = vrows[0, flip, way, slot, at:at + 1]
        send[slot, edge, DEPTH:DEPTH + 1] = speed if far else -speed
        send[slot, edge, DEPTH + 1:DEPTH + 2] = vrows[1, flip, way, slot, at:at + 1]

    def ghosts(recv):
        for way in range(2):
            for slot in range(slots):
                for far in range(2):
                    for depth in range(DEPTH):
                        at = DEPTH + tile + depth if far else DEPTH - 1 - depth
                        pad[way, slot, at:at + 1] = recv[slot, 2 * way + far, depth:depth + 1]

    wide[...] = jnp.zeros(wide.shape, jnp.float32)
    wide[0:nf * tile, 0:breadth] = tr[...]
    first = wide[0:nf * tile]
    lay(first)
    for i in range(2):
        wide[(nf + i) * tile:(nf + i + 1) * tile, 0:breadth] = vel[i]
    wide[(nf + 2) * tile:(nf + 3) * tile, 0:breadth] = land[...].astype(jnp.float32)
    along_col = wide[nf * tile:(nf + 1) * tile]
    along_row = wide[(nf + 1) * tile:(nf + 2) * tile]
    ocean = wide[(nf + 2) * tile:(nf + 3) * tile]
    for kind, (by_row, by_col) in enumerate(((along_row, along_col), (ocean, ocean))):
        both = (to_rows([by_row] * nf), to_cols(jnp.concatenate([by_col] * nf, 0)))
        for way in range(2):
            for slot in range(slots):
                x = both[way][slot]
                vrows[kind, 0, way, slot] = x
                vrows[kind, 1, way, slot] = reverse(x)
                (vpad, opad)[kind][way, slot, DEPTH:DEPTH + tile] = x

    pl.semaphore_wait(barrier, count)
    exchange(0, send1, recv1, fill_all)

    def biology(fields):
        result = [None] * nf
        for level in range(levels):
            n, p, z, d = (fields[t * levels + level] for t in range(4))
            g, kn, r, kp, lp, lz, m = (bio[level, k] for k in range(7))
            uptake = g * p * n * n / (kn * kn + n * n)
            grazing = r * z * p * p / (kp * kp + p * p)
            death = lp * p
            crowding = lz * z * z
            returned = m * d
            result[level] = returned - uptake
            result[levels + level] = uptake - grazing - death
            result[2 * levels + level] = assimilated * grazing - crowding
            result[3 * levels + level] = (1.0 - assimilated) * grazing + death + crowding - returned
        return result

    def rate(stacked, sources):
        by_way = []
        for way in range(2):
            per_slot = []
            for slot in range(slots):
                behind = pad[way, slot, 0:tile + 1]
                current = pad[way, slot, 1:tile + 2]
                beyond = pad[way, slot, 2:tile + 3]
                further = pad[way, slot, 3:tile + 4]
                low, high = jnp.minimum(current, beyond), jnp.maximum(current, beyond)
                rising = (5.0 * current + 2.0 * beyond - behind) * (1.0 / 6.0)
                falling = (5.0 * beyond + 2.0 * current - further) * (1.0 / 6.0)
                rising = jnp.minimum(jnp.maximum(rising, low), high)
                falling = jnp.minimum(jnp.maximum(falling, low), high)
                flux = ups[way, slot, 0:tile + 1] * rising + downs[way, slot, 0:tile + 1] * falling
                faces[way, slot, 0:tile + 1] = flux - mixes[way, slot, 0:tile + 1] * (beyond - current)
                per_slot.append(faces[way, slot, 0:tile] - faces[way, slot, 1:tile + 1])
            by_way.append(per_slot)
        cols = by_way[1] + [jnp.zeros((lanes - breadth, lanes), jnp.float32)]
        turned = split(jnp.concatenate(cols, 0).T)
        return [
            (turned[f] + from_rows(by_way[0], f) + sources[f]) * ocean for f in range(nf)
        ]

    sources = biology(split(first))
    arrive(0, send1, recv1)
    ghosts(recv1)
    level_of = lax.broadcasted_iota(jnp.int32, (tile + 1, lanes), 1) // tile % levels
    mixing = jnp.full((tile + 1, lanes), dif[0], jnp.float32)
    for level in range(1, levels):
        mixing = jnp.where(level_of == level, dif[level], mixing)
    for way in range(2):
        for slot in range(slots):
            for far in range(2):
                at = DEPTH + tile if far else DEPTH - 1
                sent = recv1[slot, 2 * way + far, DEPTH:DEPTH + 1]
                vpad[way, slot, at:at + 1] = -sent if far else sent
                opad[way, slot, at:at + 1] = recv1[slot, 2 * way + far, DEPTH + 1:DEPTH + 2]
            wall = opad[way, slot, 1:tile + 2] * opad[way, slot, 2:tile + 3]
            speed = 0.5 * (vpad[way, slot, 1:tile + 2] + vpad[way, slot, 2:tile + 3]) * wall
            ups[way, slot, 0:tile + 1] = jnp.maximum(speed, 0.0)
            downs[way, slot, 0:tile + 1] = jnp.minimum(speed, 0.0)
            mixes[way, slot, 0:tile + 1] = mixing * wall
    rates = rate(first, sources)
    sectioned = first + step_size * jnp.concatenate(rates, 0)
    lay(sectioned)
    exchange(1, send2, recv2, fill_tracers)
    sources = biology(split(sectioned))
    arrive(1, send2, recv2)
    ghosts(recv2)
    rates = rate(sectioned, sources)
    second = sectioned + step_size * jnp.concatenate(rates, 0)
    averaged = 0.5 * (first + second)
    held = lax.broadcasted_iota(jnp.int32, averaged.shape, 1) // tile < used
    averaged = jnp.where(held, averaged, 0.0)
    out[...] = averaged[:, 0:breadth]
    arrive(0, send1, recv1, sent=True)
    arrive(1, send2, recv2, sent=True)


def shards(gx_count, gy_count, tracers, velocity, land_mask, diffusivity, bio_rates):
    species, levels, tile, breadth = tracers.shape
    slots = breadth // tile
    nf = species * levels
    lanes = nf * tile
    height = tile + 2 * DEPTH + 4
    both = (2, slots, height, lanes)
    f32 = jnp.float32
    out = pl.pallas_call(
        functools.partial(kernel, gx_count, gy_count, slots, species, levels, tile),
        out_shape=jax.ShapeDtypeStruct((nf * tile, breadth), f32),
        in_specs=[pl.BlockSpec(memory_space=pl.ANY)] * 5,
        out_specs=pl.BlockSpec(memory_space=pltpu.VMEM),
        scratch_shapes=[
            pltpu.VMEM((nf * tile, breadth), f32),
            pltpu.VMEM((2, tile, breadth), f32),
            pltpu.VMEM((tile, breadth), jnp.int32),
            pltpu.SMEM((levels,), f32),
            pltpu.SMEM((levels, 7), f32),
            pltpu.VMEM(((nf + 3) * tile, lanes), f32),
            pltpu.VMEM((2, 2, slots, tile, lanes), f32),
            pltpu.VMEM((2, 2, 2, slots, tile, lanes), f32),
            pltpu.VMEM(both, f32),
            pltpu.VMEM(both, f32),
            pltpu.VMEM(both, f32),
            pltpu.VMEM(both, f32),
            pltpu.VMEM(both, f32),
            pltpu.VMEM(both, f32),
            pltpu.VMEM(both, f32),
            pltpu.VMEM((slots, 4, DEPTH + 2, lanes), f32),
            pltpu.VMEM((slots, 4, DEPTH + 2, lanes), f32),
            pltpu.VMEM((slots, 4, DEPTH, lanes), f32),
            pltpu.VMEM((slots, 4, DEPTH, lanes), f32),
            pltpu.SemaphoreType.DMA((5,)),
            pltpu.SemaphoreType.DMA((2, slots, 4)),
            pltpu.SemaphoreType.DMA((2, slots, 4)),
        ],
        compiler_params=pltpu.CompilerParams(collective_id=0, has_side_effects=True),
        name="tracer_step",
    )(tracers.reshape(nf * tile, breadth), velocity, land_mask, diffusivity, bio_rates.T)
    return out.reshape(tracers.shape)


def solution(mesh):
    return jax.shard_map(
        functools.partial(shards, mesh.shape["gx"], mesh.shape["gy"]),
        mesh=mesh,
        in_specs=(P(None, None, "gx", "gy"), P(None, "gx", "gy"), P("gx", "gy"), P(), P()),
        out_specs=P(None, None, "gx", "gy"),
        check_vma=False,
    )
```

```python
import functools

import jax
import jax.numpy as jnp
from jax import lax
from jax.experimental import pallas as pl
from jax.experimental.pallas import tpu as pltpu
from jax.sharding import PartitionSpec as P

step_size = 0.5
assimilated = 0.3
SEAM_TABLE = (
    ((4, 1, 0), (5, 0, 0), (3, 3, 0), (1, 2, 0)),
    ((4, 3, 1), (5, 3, 0), (0, 3, 0), (2, 2, 0)),
    ((4, 0, 1), (5, 1, 1), (1, 3, 0), (3, 2, 0)),
    ((4, 2, 0), (5, 2, 1), (2, 3, 0), (0, 2, 0)),
    ((2, 0, 1), (0, 0, 0), (3, 0, 0), (1, 0, 1)),
    ((0, 1, 0), (2, 1, 1), (3, 1, 1), (1, 1, 0)),
)
DEPTH = 2


def neighbours(gx, gy, gx_count, gy_count, slot_count, greet):
    side_tiles = gx_count
    all_columns = 6 * side_tiles
    first = lax.div(gy * all_columns + gy_count - 1, gy_count)
    used = lax.div((gy + 1) * all_columns + gy_count - 1, gy_count) - first
    table = []
    for slot in range(slot_count):
        column = jnp.minimum(first + slot, all_columns - 1)
        face = lax.div(column, side_tiles)
        b = column - face * side_tiles
        row = []
        for edge in range(4):
            codes = [t[edge][0] * 8 + t[edge][1] * 2 + t[edge][2] for t in SEAM_TABLE]
            code = jnp.int32(codes[5])
            for f in range(5):
                code = jnp.where(face == f, jnp.int32(codes[f]), code)
            t_face = lax.shift_right_logical(code, jnp.int32(3))
            t_side = lax.shift_right_logical(code, jnp.int32(1)) & 3
            t_flip = code & 1
            along = b if edge < 2 else gx
            t_along = jnp.where(t_flip == 1, side_tiles - 1 - along, along)
            t_far = jnp.where((t_side & 1) == 1, side_tiles - 1, 0)
            t_row = jnp.where(t_side < 2, t_far, t_along)
            t_col = jnp.where(t_side < 2, t_along, t_far)
            if edge == 0:
                inside, i_row, i_col = gx > 0, gx - 1, b
            elif edge == 1:
                inside, i_row, i_col = gx < side_tiles - 1, gx + 1, b
            elif edge == 2:
                inside, i_row, i_col = b > 0, gx, b - 1
            else:
                inside, i_row, i_col = b < side_tiles - 1, gx, b + 1
            t_row = jnp.where(inside, i_row, t_row)
            t_column = jnp.where(inside, face * side_tiles + i_col, t_face * side_tiles + t_col)
            t_edge = jnp.where(inside, edge ^ 1, t_side)
            flip = jnp.where(inside, 0, t_flip)
            t_gy = lax.div(t_column * gy_count, all_columns)
            t_slot = t_column - lax.div(t_gy * all_columns + gy_count - 1, gy_count)
            valid = slot < used
            local = (t_row == gx) & (t_gy == gy)
            greet(t_row, t_gy, valid & ~local)
            row.append((t_row, t_gy, t_slot, t_edge, flip, valid, local))
        table.append(row)
    return used, table


def kernel(
    gx_count, gy_count, slots, species, levels, tile,
    tr_hbm, vel_hbm, land_hbm, dif_hbm, bio_hbm, out,
    tr, vel, land, dif, bio,
    wide, rows, vrows, pad, vpad, opad, ups, downs, mixes, faces,
    send1, recv1, send2, recv2,
    in_sem, send_sem, recv_sem,
):
    gx, gy = lax.axis_index("gx"), lax.axis_index("gy")
    nf = species * levels
    lanes = nf * tile
    breadth = slots * tile
    loads = [
        pltpu.make_async_copy(src, dst, in_sem.at[i])
        for i, (src, dst) in enumerate(
            ((tr_hbm, tr), (vel_hbm, vel), (land_hbm, land), (dif_hbm, dif), (bio_hbm, bio))
        )
    ]
    barrier = pltpu.get_barrier_semaphore()

    def greet(t_row, t_gy, remote):
        @pl.when(remote)
        def _():
            pl.semaphore_signal(
                barrier, inc=1, device_id=(t_row, t_gy),
                device_id_type=pl.DeviceIdType.MESH,
            )

    used, table = neighbours(gx, gy, gx_count, gy_count, slots, greet)
    for load in loads:
        load.start()
    count = jnp.int32(0)
    for slot in range(slots):
        for edge in range(4):
            valid, local = table[slot][edge][5:]
            count = count + jnp.where(valid & ~local, 1, 0)
    for load in loads:
        load.wait()

    lane = lax.broadcasted_iota(jnp.int32, (tile, lanes), 1)
    block = lane // tile
    backward = block * tile + (tile - 1) - lane % tile

    def roll(x, shift):
        return x if shift % lanes == 0 else pltpu.roll(x, shift % lanes, 1)

    def reverse(x):
        return jnp.take_along_axis(x, backward, axis=1)

    def to_rows(fields):
        result = []
        for slot in range(slots):
            acc = roll(fields[0], -slot * tile)
            for f in range(1, len(fields)):
                acc = jnp.where(block == f, roll(fields[f], f * tile - slot * tile), acc)
            result.append(acc)
        return result

    def from_rows(per_slot, f):
        acc = roll(per_slot[0], -f * tile)
        for slot in range(1, slots):
            acc = jnp.where(block == slot, roll(per_slot[slot], slot * tile - f * tile), acc)
        return acc

    def to_cols(stacked):
        turned = stacked.T
        return [turned[s * tile:(s + 1) * tile] for s in range(slots)]

    def split(stacked):
        return [stacked[f * tile:(f + 1) * tile] for f in range(nf)]

    def exchange(stage, send, recv, fill):
        for slot in range(slots):
            for edge in range(4):
                t_row, t_gy, t_slot, t_edge, flip, valid, local = table[slot][edge]
                fill(send, slot, edge, flip)

                @pl.when(valid & ~local)
                def _():
                    pltpu.make_async_remote_copy(
                        src_ref=send.at[slot, edge], dst_ref=recv.at[t_slot, t_edge],
                        send_sem=send_sem.at[stage, slot, edge],
                        recv_sem=recv_sem.at[stage, t_slot, t_edge],
                        device_id=(t_row, t_gy), device_id_type=pl.DeviceIdType.MESH,
                    ).start()

                @pl.when(valid & local)
                def _():
                    recv[t_slot, t_edge] = send[slot, edge]

                @pl.when(~valid)
                def _():
                    recv[slot, edge] = jnp.zeros(recv.shape[2:], jnp.float32)

    def arrive(stage, send, recv, sent=False):
        for slot in range(slots):
            for edge in range(4):
                t_row, t_gy, _, _, _, valid, local = table[slot][edge]

                @pl.when(valid & ~local)
                def _():
                    copy = pltpu.make_async_remote_copy(
                        src_ref=send.at[slot, edge], dst_ref=recv.at[slot, edge],
                        send_sem=send_sem.at[stage, slot, edge],
                        recv_sem=recv_sem.at[stage, slot, edge],
                        device_id=(t_row, t_gy), device_id_type=pl.DeviceIdType.MESH,
                    )
                    if sent:
                        copy.wait_send()
                    else:
                        copy.wait_recv()

    def lay(stacked):
        both = (to_rows(split(stacked)), to_cols(stacked))
        for way in range(2):
            for slot in range(slots):
                x = both[way][slot]
                rows[0, way, slot] = x
                rows[1, way, slot] = reverse(x)
                pad[way, slot, DEPTH:DEPTH + tile] = x

    def fill_tracers(send, slot, edge, flip):
        way, far = edge // 2, edge % 2
        for depth in range(DEPTH):
            at = tile - 1 - depth if far else depth
            send[slot, edge, depth:depth + 1] = rows[flip, way, slot, at:at + 1]

    def fill_all(send, slot, edge, flip):
        fill_tracers(send, slot, edge, flip)
        way, far = edge // 2, edge % 2
        at = tile - 1 if far else 0
        speed = vrows[0, flip, way, slot, at:at + 1]
        send[slot, edge, DEPTH:DEPTH + 1] = speed if far else -speed
        send[slot, edge, DEPTH + 1:DEPTH + 2] = vrows[1, flip, way, slot, at:at + 1]

    def ghosts(recv):
        for way in range(2):
            for slot in range(slots):
                for far in range(2):
                    for depth in range(DEPTH):
                        at = DEPTH + tile + depth if far else DEPTH - 1 - depth
                        pad[way, slot, at:at + 1] = recv[slot, 2 * way + far, depth:depth + 1]

    wide[...] = jnp.zeros(wide.shape, jnp.float32)
    wide[0:nf * tile, 0:breadth] = tr[...]
    first = wide[0:nf * tile]
    lay(first)
    for i in range(2):
        wide[(nf + i) * tile:(nf + i + 1) * tile, 0:breadth] = vel[i]
    wide[(nf + 2) * tile:(nf + 3) * tile, 0:breadth] = land[...].astype(jnp.float32)
    along_col = wide[nf * tile:(nf + 1) * tile]
    along_row = wide[(nf + 1) * tile:(nf + 2) * tile]
    ocean = wide[(nf + 2) * tile:(nf + 3) * tile]
    for kind, (by_row, by_col) in enumerate(((along_row, along_col), (ocean, ocean))):
        both = (to_rows([by_row] * nf), to_cols(jnp.concatenate([by_col] * nf, 0)))
        for way in range(2):
            for slot in range(slots):
                x = both[way][slot]
                vrows[kind, 0, way, slot] = x
                vrows[kind, 1, way, slot] = reverse(x)
                (vpad, opad)[kind][way, slot, DEPTH:DEPTH + tile] = x

    pl.semaphore_wait(barrier, count)
    exchange(0, send1, recv1, fill_all)

    def biology(fields):
        result = [None] * nf
        for level in range(levels):
            n, p, z, d = (fields[t * levels + level] for t in range(4))
            g, kn, r, kp, lp, lz, m = (bio[level, k] for k in range(7))
            uptake = g * p * n * n / (kn * kn + n * n)
            grazing = r * z * p * p / (kp * kp + p * p)
            death = lp * p
            crowding = lz * z * z
            returned = m * d
            result[level] = returned - uptake
            result[levels + level] = uptake - grazing - death
            result[2 * levels + level] = assimilated * grazing - crowding
            result[3 * levels + level] = (1.0 - assimilated) * grazing + death + crowding - returned
        return result

    def rate(stacked, sources):
        by_way = []
        for way in range(2):
            per_slot = []
            for slot in range(slots):
                behind = pad[way, slot, 0:tile + 1]
                current = pad[way, slot, 1:tile + 2]
                beyond = pad[way, slot, 2:tile + 3]
                further = pad[way, slot, 3:tile + 4]
                low, high = jnp.minimum(current, beyond), jnp.maximum(current, beyond)
                rising = (5.0 * current + 2.0 * beyond - behind) * (1.0 / 6.0)
                falling = (5.0 * beyond + 2.0 * current - further) * (1.0 / 6.0)
                rising = jnp.minimum(jnp.maximum(rising, low), high)
                falling = jnp.minimum(jnp.maximum(falling, low), high)
                flux = ups[way, slot, 0:tile + 1] * rising + downs[way, slot, 0:tile + 1] * falling
                faces[way, slot, 0:tile + 1] = flux - mixes[way, slot, 0:tile + 1] * (beyond - current)
                per_slot.append(faces[way, slot, 0:tile] - faces[way, slot, 1:tile + 1])
            by_way.append(per_slot)
        cols = by_way[1] + [jnp.zeros((lanes - breadth, lanes), jnp.float32)]
        turned = split(jnp.concatenate(cols, 0).T)
        return [
            (turned[f] + from_rows(by_way[0], f) + sources[f]) * ocean for f in range(nf)
        ]

    sources = biology(split(first))
    arrive(0, send1, recv1)
    ghosts(recv1)
    level_of = lax.broadcasted_iota(jnp.int32, (tile + 1, lanes), 1) // tile % levels
    mixing = jnp.full((tile + 1, lanes), dif[0], jnp.float32)
    for level in range(1, levels):
        mixing = jnp.where(level_of == level, dif[level], mixing)
    for way in range(2):
        for slot in range(slots):
            for far in range(2):
                at = DEPTH + tile if far else DEPTH - 1
                sent = recv1[slot, 2 * way + far, DEPTH:DEPTH + 1]
                vpad[way, slot, at:at + 1] = -sent if far else sent
                opad[way, slot, at:at + 1] = recv1[slot, 2 * way + far, DEPTH + 1:DEPTH + 2]
            wall = opad[way, slot, 1:tile + 2] * opad[way, slot, 2:tile + 3]
            speed = 0.5 * (vpad[way, slot, 1:tile + 2] + vpad[way, slot, 2:tile + 3]) * wall
            ups[way, slot, 0:tile + 1] = jnp.maximum(speed, 0.0)
            downs[way, slot, 0:tile + 1] = jnp.minimum(speed, 0.0)
            mixes[way, slot, 0:tile + 1] = mixing * wall
    rates = rate(first, sources)
    sectioned = first + step_size * jnp.concatenate(rates, 0)
    lay(sectioned)
    exchange(1, send2, recv2, fill_tracers)
    sources = biology(split(sectioned))
    arrive(1, send2, recv2)
    ghosts(recv2)
    rates = rate(sectioned, sources)
    second = sectioned + step_size * jnp.concatenate(rates, 0)
    averaged = 0.5 * (first + second)
    held = lax.broadcasted_iota(jnp.int32, averaged.shape, 1) // tile < used
    averaged = jnp.where(held, averaged, 0.0)
    out[...] = averaged[:, 0:breadth]
    arrive(0, send1, recv1, sent=True)
    arrive(1, send2, recv2, sent=True)


def shards(gx_count, gy_count, tracers, velocity, land_mask, diffusivity, bio_rates):
    species, levels, tile, breadth = tracers.shape
    slots = breadth // tile
    nf = species * levels
    lanes = nf * tile
    height = tile + 2 * DEPTH + 4
    both = (2, slots, height, lanes)
    f32 = jnp.float32
    out = pl.pallas_call(
        functools.partial(kernel, gx_count, gy_count, slots, species, levels, tile),
        out_shape=jax.ShapeDtypeStruct((nf * tile, breadth), f32),
        in_specs=[pl.BlockSpec(memory_space=pltpu.HBM)] * 5,
        out_specs=pl.BlockSpec(memory_space=pltpu.VMEM),
        scratch_shapes=[
            pltpu.VMEM((nf * tile, breadth), f32),
            pltpu.VMEM((2, tile, breadth), f32),
            pltpu.VMEM((tile, breadth), jnp.int32),
            pltpu.SMEM((levels,), f32),
            pltpu.SMEM((levels, 7), f32),
            pltpu.VMEM(((nf + 3) * tile, lanes), f32),
            pltpu.VMEM((2, 2, slots, tile, lanes), f32),
            pltpu.VMEM((2, 2, 2, slots, tile, lanes), f32),
            pltpu.VMEM(both, f32),
            pltpu.VMEM(both, f32),
            pltpu.VMEM(both, f32),
            pltpu.VMEM(both, f32),
            pltpu.VMEM(both, f32),
            pltpu.VMEM(both, f32),
            pltpu.VMEM(both, f32),
            pltpu.VMEM((slots, 4, DEPTH + 2, lanes), f32),
            pltpu.VMEM((slots, 4, DEPTH + 2, lanes), f32),
            pltpu.VMEM((slots, 4, DEPTH, lanes), f32),
            pltpu.VMEM((slots, 4, DEPTH, lanes), f32),
            pltpu.SemaphoreType.DMA((5,)),
            pltpu.SemaphoreType.DMA((2, slots, 4)),
            pltpu.SemaphoreType.DMA((2, slots, 4)),
        ],
        compiler_params=pltpu.CompilerParams(collective_id=0, has_side_effects=True, vmem_limit_bytes=16 * 1024 * 1024),
        name="tracer_step",
    )(*(
        pltpu.with_memory_space_constraint(x, pltpu.HBM)
        for x in (tracers.reshape(nf * tile, breadth), velocity, land_mask, diffusivity, bio_rates.T)
    ))
    return out.reshape(tracers.shape)


def solution(mesh):
    return jax.shard_map(
        functools.partial(shards, mesh.shape["gx"], mesh.shape["gy"]),
        mesh=mesh,
        in_specs=(P(None, None, "gx", "gy"), P(None, "gx", "gy"), P("gx", "gy"), P(), P()),
        out_specs=P(None, None, "gx", "gy"),
        check_vma=False,
    )
```

```python
import functools

import jax
import jax.numpy as jnp
from jax import lax
from jax.experimental import pallas as pl
from jax.experimental.pallas import tpu as pltpu
from jax.sharding import PartitionSpec as P

step_size = 0.5
assimilated = 0.3
SEAM_TABLE = (
    ((4, 1, 0), (5, 0, 0), (3, 3, 0), (1, 2, 0)),
    ((4, 3, 1), (5, 3, 0), (0, 3, 0), (2, 2, 0)),
    ((4, 0, 1), (5, 1, 1), (1, 3, 0), (3, 2, 0)),
    ((4, 2, 0), (5, 2, 1), (2, 3, 0), (0, 2, 0)),
    ((2, 0, 1), (0, 0, 0), (3, 0, 0), (1, 0, 1)),
    ((0, 1, 0), (2, 1, 1), (3, 1, 1), (1, 1, 0)),
)
DEPTH = 2


def neighbours(gx, gy, gx_count, gy_count, slot_count, greet):
    side_tiles = gx_count
    all_columns = 6 * side_tiles
    first = lax.div(gy * all_columns + gy_count - 1, gy_count)
    used = lax.div((gy + 1) * all_columns + gy_count - 1, gy_count) - first
    table = []
    for slot in range(slot_count):
        column = jnp.minimum(first + slot, all_columns - 1)
        face = lax.div(column, side_tiles)
        b = column - face * side_tiles
        row = []
        for edge in range(4):
            codes = [t[edge][0] * 8 + t[edge][1] * 2 + t[edge][2] for t in SEAM_TABLE]
            code = jnp.int32(codes[5])
            for f in range(5):
                code = jnp.where(face == f, jnp.int32(codes[f]), code)
            t_face = lax.shift_right_logical(code, jnp.int32(3))
            t_side = lax.shift_right_logical(code, jnp.int32(1)) & 3
            t_flip = code & 1
            along = b if edge < 2 else gx
            t_along = jnp.where(t_flip == 1, side_tiles - 1 - along, along)
            t_far = jnp.where((t_side & 1) == 1, side_tiles - 1, 0)
            t_row = jnp.where(t_side < 2, t_far, t_along)
            t_col = jnp.where(t_side < 2, t_along, t_far)
            if edge == 0:
                inside, i_row, i_col = gx > 0, gx - 1, b
            elif edge == 1:
                inside, i_row, i_col = gx < side_tiles - 1, gx + 1, b
            elif edge == 2:
                inside, i_row, i_col = b > 0, gx, b - 1
            else:
                inside, i_row, i_col = b < side_tiles - 1, gx, b + 1
            t_row = jnp.where(inside, i_row, t_row)
            t_column = jnp.where(inside, face * side_tiles + i_col, t_face * side_tiles + t_col)
            t_edge = jnp.where(inside, edge ^ 1, t_side)
            flip = jnp.where(inside, 0, t_flip)
            t_gy = lax.div(t_column * gy_count, all_columns)
            t_slot = t_column - lax.div(t_gy * all_columns + gy_count - 1, gy_count)
            valid = slot < used
            local = (t_row == gx) & (t_gy == gy)
            greet(t_row, t_gy, valid & ~local)
            row.append((t_row, t_gy, t_slot, t_edge, flip, valid, local))
        table.append(row)
    return used, table


def kernel(
    gx_count, gy_count, slots, species, levels, tile,
    tr_hbm, vel_hbm, land_hbm, dif_hbm, bio_hbm, out,
    tr, vel, land, dif, bio,
    wide, rows, vrows, pad, vpad, opad, ups, downs, mixes, faces,
    send1, recv1, send2, recv2,
    in_sem, send_sem, recv_sem,
):
    gx, gy = lax.axis_index("gx"), lax.axis_index("gy")
    nf = species * levels
    lanes = nf * tile
    breadth = slots * tile
    loads = [
        pltpu.make_async_copy(src, dst, in_sem.at[i])
        for i, (src, dst) in enumerate(
            ((tr_hbm, tr), (vel_hbm, vel), (land_hbm, land), (dif_hbm, dif), (bio_hbm, bio))
        )
    ]
    barrier = pltpu.get_barrier_semaphore()

    def greet(t_row, t_gy, remote):
        @pl.when(remote)
        def _():
            pl.semaphore_signal(
                barrier, inc=1, device_id=(t_row, t_gy),
                device_id_type=pl.DeviceIdType.MESH,
            )

    used, table = neighbours(gx, gy, gx_count, gy_count, slots, greet)
    for load in loads:
        load.start()
    count = jnp.int32(0)
    for slot in range(slots):
        for edge in range(4):
            valid, local = table[slot][edge][5:]
            count = count + jnp.where(valid & ~local, 1, 0)
    for load in loads:
        load.wait()

    lane = lax.broadcasted_iota(jnp.int32, (tile, lanes), 1)
    block = lane // tile
    backward = block * tile + (tile - 1) - lane % tile

    def roll(x, shift):
        return x if shift % lanes == 0 else pltpu.roll(x, shift % lanes, 1)

    def reverse(x):
        return jnp.take_along_axis(x, backward, axis=1)

    def to_rows(fields):
        result = []
        for slot in range(slots):
            acc = roll(fields[0], -slot * tile)
            for f in range(1, len(fields)):
                acc = jnp.where(block == f, roll(fields[f], f * tile - slot * tile), acc)
            result.append(acc)
        return result

    def from_rows(per_slot, f):
        acc = roll(per_slot[0], -f * tile)
        for slot in range(1, slots):
            acc = jnp.where(block == slot, roll(per_slot[slot], slot * tile - f * tile), acc)
        return acc

    def to_cols(stacked):
        turned = stacked.T
        return [turned[s * tile:(s + 1) * tile] for s in range(slots)]

    def split(stacked):
        return [stacked[f * tile:(f + 1) * tile] for f in range(nf)]

    def exchange(stage, send, recv, fill, ready=None):
        if ready is not None:
            for slot in range(slots):
                for edge in range(4):
                    fill(send, slot, edge, table[slot][edge][4])
            ready()
        for slot in range(slots):
            for edge in range(4):
                t_row, t_gy, t_slot, t_edge, flip, valid, local = table[slot][edge]
                if ready is None:
                    fill(send, slot, edge, flip)

                @pl.when(valid & ~local)
                def _():
                    pltpu.make_async_remote_copy(
                        src_ref=send.at[slot, edge], dst_ref=recv.at[t_slot, t_edge],
                        send_sem=send_sem.at[stage, slot, edge],
                        recv_sem=recv_sem.at[stage, t_slot, t_edge],
                        device_id=(t_row, t_gy), device_id_type=pl.DeviceIdType.MESH,
                    ).start()

                @pl.when(valid & local)
                def _():
                    recv[t_slot, t_edge] = send[slot, edge]

                @pl.when(~valid)
                def _():
                    recv[slot, edge] = jnp.zeros(recv.shape[2:], jnp.float32)

    def arrive(stage, send, recv, sent=False):
        for slot in range(slots):
            for edge in range(4):
                t_row, t_gy, _, _, _, valid, local = table[slot][edge]

                @pl.when(valid & ~local)
                def _():
                    copy = pltpu.make_async_remote_copy(
                        src_ref=send.at[slot, edge], dst_ref=recv.at[slot, edge],
                        send_sem=send_sem.at[stage, slot, edge],
                        recv_sem=recv_sem.at[stage, slot, edge],
                        device_id=(t_row, t_gy), device_id_type=pl.DeviceIdType.MESH,
                    )
                    if sent:
                        copy.wait_send()
                    else:
                        copy.wait_recv()

    def lay(stacked):
        both = (to_rows(split(stacked)), to_cols(stacked))
        for way in range(2):
            for slot in range(slots):
                x = both[way][slot]
                rows[0, way, slot] = x
                rows[1, way, slot] = reverse(x)
                pad[way, slot, DEPTH:DEPTH + tile] = x

    def fill_tracers(send, slot, edge, flip):
        way, far = edge // 2, edge % 2
        for depth in range(DEPTH):
            at = tile - 1 - depth if far else depth
            send[slot, edge, depth:depth + 1] = rows[flip, way, slot, at:at + 1]

    def fill_all(send, slot, edge, flip):
        fill_tracers(send, slot, edge, flip)
        way, far = edge // 2, edge % 2
        at = tile - 1 if far else 0
        speed = vrows[0, flip, way, slot, at:at + 1]
        send[slot, edge, DEPTH:DEPTH + 1] = speed if far else -speed
        send[slot, edge, DEPTH + 1:DEPTH + 2] = vrows[1, flip, way, slot, at:at + 1]

    def ghosts(recv):
        for way in range(2):
            for slot in range(slots):
                for far in range(2):
                    for depth in range(DEPTH):
                        at = DEPTH + tile + depth if far else DEPTH - 1 - depth
                        pad[way, slot, at:at + 1] = recv[slot, 2 * way + far, depth:depth + 1]

    wide[...] = jnp.zeros(wide.shape, jnp.float32)
    wide[0:nf * tile, 0:breadth] = tr[...]
    first = wide[0:nf * tile]
    lay(first)
    for i in range(2):
        wide[(nf + i) * tile:(nf + i + 1) * tile, 0:breadth] = vel[i]
    wide[(nf + 2) * tile:(nf + 3) * tile, 0:breadth] = land[...].astype(jnp.float32)
    along_col = wide[nf * tile:(nf + 1) * tile]
    along_row = wide[(nf + 1) * tile:(nf + 2) * tile]
    ocean = wide[(nf + 2) * tile:(nf + 3) * tile]
    for kind, (by_row, by_col) in enumerate(((along_row, along_col), (ocean, ocean))):
        both = (to_rows([by_row] * nf), to_cols(jnp.concatenate([by_col] * nf, 0)))
        for way in range(2):
            for slot in range(slots):
                x = both[way][slot]
                vrows[kind, 0, way, slot] = x
                vrows[kind, 1, way, slot] = reverse(x)
                (vpad, opad)[kind][way, slot, DEPTH:DEPTH + tile] = x

    exchange(0, send1, recv1, fill_all, lambda: pl.semaphore_wait(barrier, count))

    def biology(fields):
        result = [None] * nf
        for level in range(levels):
            n, p, z, d = (fields[t * levels + level] for t in range(4))
            g, kn, r, kp, lp, lz, m = (bio[level, k] for k in range(7))
            uptake = g * p * n * n / (kn * kn + n * n)
            grazing = r * z * p * p / (kp * kp + p * p)
            death = lp * p
            crowding = lz * z * z
            returned = m * d
            result[level] = returned - uptake
            result[levels + level] = uptake - grazing - death
            result[2 * levels + level] = assimilated * grazing - crowding
            result[3 * levels + level] = (1.0 - assimilated) * grazing + death + crowding - returned
        return result

    def rate(stacked, sources):
        by_way = []
        for way in range(2):
            per_slot = []
            for slot in range(slots):
                behind = pad[way, slot, 0:tile + 1]
                current = pad[way, slot, 1:tile + 2]
                beyond = pad[way, slot, 2:tile + 3]
                further = pad[way, slot, 3:tile + 4]
                low, high = jnp.minimum(current, beyond), jnp.maximum(current, beyond)
                rising = (5.0 * current + 2.0 * beyond - behind) * (1.0 / 6.0)
                falling = (5.0 * beyond + 2.0 * current - further) * (1.0 / 6.0)
                rising = jnp.minimum(jnp.maximum(rising, low), high)
                falling = jnp.minimum(jnp.maximum(falling, low), high)
                flux = ups[way, slot, 0:tile + 1] * rising + downs[way, slot, 0:tile + 1] * falling
                faces[way, slot, 0:tile + 1] = flux - mixes[way, slot, 0:tile + 1] * (beyond - current)
                per_slot.append(faces[way, slot, 0:tile] - faces[way, slot, 1:tile + 1])
            by_way.append(per_slot)
        cols = by_way[1] + [jnp.zeros((lanes - breadth, lanes), jnp.float32)]
        turned = split(jnp.concatenate(cols, 0).T)
        return [
            (turned[f] + from_rows(by_way[0], f) + sources[f]) * ocean for f in range(nf)
        ]

    sources = biology(split(first))
    arrive(0, send1, recv1)
    ghosts(recv1)
    level_of = lax.broadcasted_iota(jnp.int32, (tile + 1, lanes), 1) // tile % levels
    mixing = jnp.full((tile + 1, lanes), dif[0], jnp.float32)
    for level in range(1, levels):
        mixing = jnp.where(level_of == level, dif[level], mixing)
    for way in range(2):
        for slot in range(slots):
            for far in range(2):
                at = DEPTH + tile if far else DEPTH - 1
                sent = recv1[slot, 2 * way + far, DEPTH:DEPTH + 1]
                vpad[way, slot, at:at + 1] = -sent if far else sent
                opad[way, slot, at:at + 1] = recv1[slot, 2 * way + far, DEPTH + 1:DEPTH + 2]
            wall = opad[way, slot, 1:tile + 2] * opad[way, slot, 2:tile + 3]
            speed = 0.5 * (vpad[way, slot, 1:tile + 2] + vpad[way, slot, 2:tile + 3]) * wall
            ups[way, slot, 0:tile + 1] = jnp.maximum(speed, 0.0)
            downs[way, slot, 0:tile + 1] = jnp.minimum(speed, 0.0)
            mixes[way, slot, 0:tile + 1] = mixing * wall
    rates = rate(first, sources)
    sectioned = first + step_size * jnp.concatenate(rates, 0)
    lay(sectioned)
    exchange(1, send2, recv2, fill_tracers)
    sources = biology(split(sectioned))
    arrive(1, send2, recv2)
    ghosts(recv2)
    rates = rate(sectioned, sources)
    second = sectioned + step_size * jnp.concatenate(rates, 0)
    averaged = 0.5 * (first + second)
    held = lax.broadcasted_iota(jnp.int32, averaged.shape, 1) // tile < used
    averaged = jnp.where(held, averaged, 0.0)
    out[...] = averaged[:, 0:breadth]
    arrive(0, send1, recv1, sent=True)
    arrive(1, send2, recv2, sent=True)


def shards(gx_count, gy_count, tracers, velocity, land_mask, diffusivity, bio_rates):
    species, levels, tile, breadth = tracers.shape
    slots = breadth // tile
    nf = species * levels
    lanes = nf * tile
    height = tile + 2 * DEPTH + 4
    both = (2, slots, height, lanes)
    f32 = jnp.float32
    out = pl.pallas_call(
        functools.partial(kernel, gx_count, gy_count, slots, species, levels, tile),
        out_shape=jax.ShapeDtypeStruct((nf * tile, breadth), f32),
        in_specs=[pl.BlockSpec(memory_space=pltpu.HBM)] * 5,
        out_specs=pl.BlockSpec(memory_space=pltpu.VMEM),
        scratch_shapes=[
            pltpu.VMEM((nf * tile, breadth), f32),
            pltpu.VMEM((2, tile, breadth), f32),
            pltpu.VMEM((tile, breadth), jnp.int32),
            pltpu.SMEM((levels,), f32),
            pltpu.SMEM((levels, 7), f32),
            pltpu.VMEM(((nf + 3) * tile, lanes), f32),
            pltpu.VMEM((2, 2, slots, tile, lanes), f32),
            pltpu.VMEM((2, 2, 2, slots, tile, lanes), f32),
            pltpu.VMEM(both, f32),
            pltpu.VMEM(both, f32),
            pltpu.VMEM(both, f32),
            pltpu.VMEM(both, f32),
            pltpu.VMEM(both, f32),
            pltpu.VMEM(both, f32),
            pltpu.VMEM(both, f32),
            pltpu.VMEM((slots, 4, DEPTH + 2, lanes), f32),
            pltpu.VMEM((slots, 4, DEPTH + 2, lanes), f32),
            pltpu.VMEM((slots, 4, DEPTH, lanes), f32),
            pltpu.VMEM((slots, 4, DEPTH, lanes), f32),
            pltpu.SemaphoreType.DMA((5,)),
            pltpu.SemaphoreType.DMA((2, slots, 4)),
            pltpu.SemaphoreType.DMA((2, slots, 4)),
        ],
        compiler_params=pltpu.CompilerParams(collective_id=0, has_side_effects=True, vmem_limit_bytes=16 * 1024 * 1024),
        name="tracer_step",
    )(*(
        pltpu.with_memory_space_constraint(x, pltpu.HBM)
        for x in (tracers.reshape(nf * tile, breadth), velocity, land_mask, diffusivity, bio_rates.T)
    ))
    return out.reshape(tracers.shape)


def solution(mesh):
    return jax.shard_map(
        functools.partial(shards, mesh.shape["gx"], mesh.shape["gy"]),
        mesh=mesh,
        in_specs=(P(None, None, "gx", "gy"), P(None, "gx", "gy"), P("gx", "gy"), P(), P()),
        out_specs=P(None, None, "gx", "gy"),
        check_vma=False,
    )
```
